32 devices in a mesh: segment: 4 (over y, x), ctx: 8 (over z, core).
Axes of the slice: x: 2, y: 2, z: 4, core: 2. Of those that a mesh axis runs over, the one named last changes fastest.
Arguments:
- segment_input: bfloat16 [4, 1024, 2048], P('segment', 'ctx'), may hold values from -6 to 6
- views: bfloat16 [4, 16, 128, 384], P('segment'), may hold values from -0.5 to 0.5
- gate_vec: float32 [4, 16, 128], P('segment'), may hold values from -0.9 to 0.9
- base_rate: float32 [4, 16], P('segment'), may hold values from 0.05 to 1.5
- norm_gain: float32 [4, 16, 128], P('segment'), may hold values from 0.5 to 1.5
- init_weight: float32 [4, 16, 128, 128], P('segment'), may hold values from -0.5 to 0.5
- out_grad: bfloat16 [4, 1024, 2048], P('segment', 'ctx'), may hold values from -6 to 6
Outputs:
- next_input: bfloat16 [4, 1024, 2048], P('segment', 'ctx')
- view_grad: float32 [4, 16, 128, 384], P('segment', 'ctx')
- gate_grad: float32 [4, 16, 128], P('segment', 'ctx')
- rate_grad: float32 [4, 16], P('segment', 'ctx')
- gain_grad: float32 [4, 16, 128], P('segment', 'ctx')
- init_grad: float32 [4, 16, 128, 128], P('segment', 'ctx')
- input_grad: bfloat16 [4, 1024, 2048], P('segment', 'ctx')
The draws below stay inside these ranges and needn't reach their ends.
All inputs are finite; a program needn't handle non-finite values.
Results may differ from the reference program's by a relative error of at most 0.001.
Values may be sent and summed in bfloat16 or wider, within the bound.
A program may use at most 128 MiB of HBM per device.

```python
import math
import jax
import jax.numpy as jnp
from jax import lax

H = 16
HD = 128
MB = 16
TOKENS = 1024
SEGMENTS = 4


def steps_of(key, dims, shards, smallest, largest):
    def one(position, blocks):
        draws = jax.random.uniform(jax.random.fold_in(jax.random.fold_in(key, 6), position), (blocks,), jnp.float32, smallest / len(shards), largest / len(shards))
        return jnp.repeat(jnp.exp(draws), dims[position] // blocks).reshape((-1,) + (1,) * (len(dims) - position - 1))

    gain = one(*shards[0])
    for cut in shards[1:]:
        gain = gain * one(*cut)
    return gain


def noise(stream_key, shape, width, most, split=(), kind=jnp.bfloat16):
    values = jax.random.normal(stream_key, shape, jnp.float32) * width
    if len(split) > 0:
        values = steps_of(stream_key, shape, split, -0.22, 0.18) * values
    return jnp.clip(values, min=-most, max=most).astype(kind)


def setup_inputs(seed: int = 0) -> dict:
    key_list = jax.random.split(jax.random.key(seed), 8)
    segment_input = noise(key_list[0], (SEGMENTS, TOKENS, H * HD), 1.0, 6.0, ((0, 4), (1, 8)))
    views = noise(key_list[1], (SEGMENTS, H, HD, 3 * HD), HD ** -0.5, 0.5, ((0, 4),))
    gate_vec = noise(key_list[2], (SEGMENTS, H, HD), 0.15, 0.9, ((0, 4),), jnp.float32)
    base_rate = jnp.clip(jnp.exp(math.log(1.5) - 3.4011974 * jax.random.uniform(key_list[3], (SEGMENTS, H), jnp.float32) ** steps_of(key_list[3], (SEGMENTS, H), ((0, 4),), -0.2, 0.2)), 0.05, 1.5)
    norm_gain = jnp.clip(1.0 + 0.1 * jax.random.normal(key_list[4], (SEGMENTS, H, HD), jnp.float32), 0.5, 1.5)
    init_weight = noise(key_list[5], (SEGMENTS, H, HD, HD), HD ** -0.5, 0.5, ((0, 4),), jnp.float32)
    out_grad = noise(key_list[6], (SEGMENTS, TOKENS, H * HD), 1.0, 6.0, ((0, 4), (1, 8)))
    return dict(segment_input=segment_input, views=views, gate_vec=gate_vec, base_rate=base_rate, norm_gain=norm_gain, init_weight=init_weight, out_grad=out_grad)


HIGH = lax.Precision.HIGHEST

def head_views(view_f, gate_f, rate_f, tokens_f):
    tok_count = tokens_f.shape[0]
    head_count, head_width = gate_f.shape
    pieces = tokens_f.reshape(tok_count, head_count, head_width)
    packed = jnp.einsum('thd,hde->hte', pieces, view_f, precision=HIGH)
    queries = packed[:, :, :head_width]
    raw_keys = packed[:, :, head_width:2 * head_width]
    values = packed[:, :, 2 * head_width:]
    keys_norm = raw_keys * lax.rsqrt(lax.optimization_barrier(jnp.mean(raw_keys * raw_keys, axis=-1, keepdims=True)) + 1e-06)
    targets = values - keys_norm
    logits = jnp.einsum('thd,hd->ht', pieces, gate_f, precision=HIGH)
    rates = rate_f[:, None] * jax.nn.sigmoid(logits) / (MB * head_width)
    return (queries, keys_norm, targets, rates)

def blocked(array):
    head_count, tok_count = array.shape[:2]
    shaped = array.reshape((head_count, tok_count // MB, MB) + array.shape[2:])
    return jnp.moveaxis(shaped, 1, 0)

def run_chain(queries, keys_norm, targets, rates, start_weight):
    causal = jnp.tril(jnp.ones((MB, MB), queries.dtype))

    def minibatch_step(weight, blocks):
        q_block, k_block, y_block, e_block = blocks
        residual = jnp.einsum('hbd,hde->hbe', k_block, weight, precision=HIGH) - y_block
        scores = jnp.einsum('hbd,hcd->hbc', q_block, k_block, precision=HIGH) * causal * e_block[:, None, :]
        output = jnp.einsum('hbd,hde->hbe', q_block, weight, precision=HIGH) - jnp.einsum('hbc,hce->hbe', scores, residual, precision=HIGH)
        weight_next = weight - jnp.einsum('hbd,hbe->hde', k_block * e_block[:, :, None], residual, precision=HIGH)
        return (weight_next, output)
    blocks = (blocked(queries), blocked(keys_norm), blocked(targets), blocked(rates))
    end_weight, outputs = lax.scan(minibatch_step, start_weight, blocks)
    head_count, tok_count, head_width = queries.shape
    outputs = jnp.moveaxis(outputs, 0, 1).reshape(head_count, tok_count, head_width)
    return (outputs, end_weight)

def finish(tokens_f, outputs, gain_f):
    head_count, tok_count, head_width = outputs.shape
    centred = outputs - lax.optimization_barrier(jnp.mean(outputs, axis=-1, keepdims=True))
    normed = centred * lax.rsqrt(lax.optimization_barrier(jnp.mean(centred * centred, axis=-1, keepdims=True)) + 1e-05)
    mixed = normed * gain_f[:, None, :]
    return tokens_f + jnp.moveaxis(mixed, 0, 1).reshape(tok_count, head_count * head_width)

def reference(segment_input, views, gate_vec, base_rate, norm_gain, init_weight, out_grad):

    def section(packed):
        tokens, view_w, gate_w, rate_w, gain_w, start_w, cotangent = packed

        def forward(view_f, gate_f, rate_f, gain_f, start_f, tokens_f):
            queries, keys_norm, targets, rates = head_views(view_f, gate_f, rate_f, tokens_f)
            outputs, end_weight = run_chain(queries, keys_norm, targets, rates, start_f)
            return finish(tokens_f, outputs, gain_f)
        result, pullback = jax.vjp(forward, view_w.astype(jnp.float32), gate_w, rate_w, gain_w, start_w, tokens.astype(jnp.float32))
        grads = pullback(cotangent.astype(jnp.float32))
        return (result.astype(jnp.bfloat16), grads[0], grads[1], grads[2], grads[3], grads[4], grads[5].astype(jnp.bfloat16))
    outs = lax.map(section, (segment_input, views, gate_vec, base_rate, norm_gain, init_weight, out_grad))
    next_input = jnp.roll(outs[0], 1, axis=0)
    input_grad = jnp.roll(outs[6], -1, axis=0)
    return (next_input, outs[1], outs[2], outs[3], outs[4], outs[5], input_grad)
```

```python
import functools

import jax
import jax.numpy as jnp
from jax import lax
from jax.experimental import pallas as pl
from jax.experimental.pallas import tpu as pltpu
from jax.sharding import PartitionSpec as P

MB = 16
F32 = jnp.float32
BF16 = jnp.bfloat16
NN = (((1,), (0,)), ((), ()))
NT = (((1,), (1,)), ((), ()))
TN = (((0,), (0,)), ((), ()))


def dot(left, right, dims):
    return lax.dot_general(left, right, dims, preferred_element_type=F32)


def split(value):
    high = value.astype(BF16)
    low = (value - high.astype(F32)).astype(BF16)
    return high, low


def cat(parts, axis):
    return jnp.concatenate(parts, axis=axis)


def stack(left, right, axis):
    return cat([left[0], right[0]], axis), cat([left[1], right[1]], axis)


def product(left, right, dims):
    left_axis, right_axis = dims[0][0][0], dims[0][1][0]
    left_both = cat(left, left_axis)
    wide = cat(right, 1 - right_axis)
    result = dot(left_both, cat([wide, wide], right_axis), dims)
    columns = result.shape[1] // 2
    return result[:, :columns] + result[:, columns:]


def row_mean(value):
    return jnp.mean(value, axis=-1, keepdims=True)


def positions(size):
    rows = lax.broadcasted_iota(jnp.int32, (size, size), 0)
    columns = lax.broadcasted_iota(jnp.int32, (size, size), 1)
    return rows, columns


def block_inverse(strict, size):
    rows, columns = positions(size)
    width = MB
    eye = jnp.where(rows == columns, 1.0, 0.0).astype(F32)
    inverse = eye
    while width < size:
        same = (rows // (2 * width)) == (columns // (2 * width))
        below = (rows // width) > (columns // width)
        corner = jnp.where(same & below, strict, 0.0)
        if width == MB:
            inverse = eye - corner
        else:
            pair = split(inverse)
            inverse = inverse - product(split(product(pair, split(corner), NN)), pair, NN)
        width *= 2
    return inverse


def kernel(
    count, heads, size, width,
    x_ref, og_ref, views_ref, gate_ref, rate_ref, gain_ref, init_ref,
    out_ref, vgrad_ref, ggrad_ref, rgrad_ref, ngrad_ref, igrad_ref, dx_ref,
    view_buf, init_buf, qs, ks, krs, qes, as_, ss, ts, fs, rs, dzs, ws, gs,
    kf, bs, sbs, os_, v0s, ls, invs, sigs, load_sem,
):
    me = lax.axis_index("ctx")
    first_head = me * heads
    loads = [
        pltpu.make_async_copy(views_ref.at[0, pl.ds(first_head, heads)], view_buf, load_sem.at[0]),
        pltpu.make_async_copy(init_ref.at[0, pl.ds(first_head, heads)], init_buf, load_sem.at[1]),
    ]
    for load in loads:
        load.start()
    for load in loads:
        load.wait()
    scale = 1.0 / (MB * width)

    def columns_of(h):
        return slice(h * width, (h + 1) * width)

    def gate_of(h):
        return gate_ref[0, pl.ds(first_head + h, 1), :]

    def gain_of(h):
        return gain_ref[0, pl.ds(first_head + h, 1), :]

    def base_of(h):
        lane = lax.broadcasted_iota(jnp.int32, rate_ref.shape, 1)
        return jnp.sum(jnp.where(lane == first_head + h, rate_ref[...], 0.0), axis=1, keepdims=True)

    def put(ref, c, h, pair):
        ref[c, h, 0] = pair[0]
        ref[c, h, 1] = pair[1]

    def get(ref, c, h):
        return ref[c, h, 0], ref[c, h, 1]

    def masks():
        rows, columns = positions(size)
        return rows >= columns, (rows // MB) > (columns // MB)

    def prepare(c, h):
        x = x_ref[c, :, columns_of(h)]
        packed = dot(x, view_buf[h], NN)
        q = packed[:, :width]
        raw = packed[:, width : 2 * width]
        inv = lax.rsqrt(row_mean(raw * raw) + 1e-06)
        k = raw * inv
        y = packed[:, 2 * width :] - k
        logit = jnp.sum(x.astype(F32) * gate_of(h), axis=-1, keepdims=True)
        sig = jax.nn.sigmoid(logit)
        kr = k * (base_of(h) * sig * scale)
        k2, q2, kr2 = split(k), split(q), split(kr)
        causal, before = masks()
        grams = product(stack(k2, q2, 0), kr2, NT)
        inverse = block_inverse(jnp.where(before, grams[:size], 0.0), size)
        scores = split(jnp.where(causal, grams[size:], 0.0))
        t2 = split(inverse)
        ab = product(t2, stack(k2, split(y), 1), NN)
        ab2 = split(ab)
        sab = product(scores, ab2, NN)
        fo = product(kr2, ab2, TN)
        put(qs, c, h, q2)
        put(ks, c, h, k2)
        put(krs, c, h, kr2)
        put(qes, c, h, split(q - sab[:, :width]))
        put(as_, c, h, (ab2[0][:, :width], ab2[1][:, :width]))
        put(ss, c, h, scores)
        put(ts, c, h, t2)
        put(fs, c, h, split(fo[:, :width]))
        kf[c, h] = k
        bs[c, h] = ab[:, width:]
        sbs[c, h] = sab[:, width:]
        os_[c, h] = fo[:, width:]
        invs[c, h] = inv
        sigs[c, h] = sig

    def advance(c, h):
        w2 = split(init_buf[h])
        put(ws, c, h, w2)
        init_buf[h] = init_buf[h] - product(get(fs, c, h), w2, NN) + os_[c, h]

    def outputs(c, h):
        cols = columns_of(h)
        qe = get(qes, c, h)
        moved = product(stack(qe, get(as_, c, h), 0), get(ws, c, h), NN)
        z = moved[:size] + sbs[c, h]
        put(rs, c, h, split(moved[size:] - bs[c, h]))
        centred = z - row_mean(z)
        rstd = lax.rsqrt(row_mean(centred * centred) + 1e-05)
        normed = centred * rstd
        gain = gain_of(h)
        out_ref[c, :, cols] = (x_ref[c, :, cols].astype(F32) + gain * normed).astype(BF16)
        dout = og_ref[c, :, cols].astype(F32)
        ngrad_ref[0, h : h + 1, :] += jnp.sum(dout * normed, axis=0, keepdims=True)
        dn = dout * gain
        dz = rstd * (dn - row_mean(dn) - normed * row_mean(dn * normed))
        dz2 = split(dz)
        put(dzs, c, h, dz2)
        back = product(stack(qe, get(ss, c, h), 1), dz2, TN)
        ls[c, h] = back[:width]
        v0s[c, h] = back[width:]

    def retreat(c, h):
        g = igrad_ref[0, h]
        g2 = split(g)
        put(gs, c, h, g2)
        igrad_ref[0, h] = g - product(get(fs, c, h), g2, TN) + ls[c, h]

    def gradients(c, h):
        cols = columns_of(h)
        g2, kr2, w2, r2, dz2 = get(gs, c, h), get(krs, c, h), get(ws, c, h), get(rs, c, h), get(dzs, c, h)
        v = v0s[c, h] + product(kr2, g2, NN)
        du = -product(get(ts, c, h), split(v), TN)
        both = stack(dz2, split(du), 0)
        causal, before = masks()
        inner = product(both, r2, NT)
        dscores = jnp.where(causal, -inner[:size], 0.0)
        dstrict = jnp.where(before, -inner[size:], 0.0)
        d2 = stack(split(dscores), split(dstrict), 0)
        dqk = product(both, w2, NT) + product(d2, kr2, NN)
        dkr = product(d2, stack(get(qs, c, h), get(ks, c, h), 0), TN) - product(r2, g2, NT)
        sig, inv, k, base = sigs[c, h], invs[c, h], kf[c, h], base_of(h)
        rate_factor = sig * scale
        dk = dqk[size:] + (base * rate_factor) * dkr + du
        draw = inv * (dk - k * row_mean(dk * k))
        drate = jnp.sum(dkr * k, axis=-1, keepdims=True) * rate_factor
        rgrad_ref[:, h : h + 1] += jnp.sum(drate, axis=0, keepdims=True)
        dlogit = drate * base * (1.0 - sig)
        x = x_ref[c, :, cols]
        ggrad_ref[0, h : h + 1, :] += jnp.sum(dlogit * x.astype(F32), axis=0, keepdims=True)
        packed = split(cat([dqk[:size], draw, -du], 1))
        vgrad_ref[0, h] += dot(cat([x, x], 0), cat(packed, 0), TN)
        views = view_buf[h]
        dx = dot(packed[0], views, NT) + dot(packed[1], views, NT)
        dx = dx + og_ref[c, :, cols].astype(F32) + dlogit * gate_of(h)
        dx_ref[c, :, cols] = dx.astype(BF16)

    for ref in (vgrad_ref, ggrad_ref, rgrad_ref, ngrad_ref, igrad_ref):
        ref[...] = jnp.zeros_like(ref)

    all_heads = range(heads)

    def forward(c, carry):
        for h in all_heads:
            prepare(c, h)
        for h in all_heads:
            advance(c, h)
        for h in all_heads:
            outputs(c, h)
        return carry

    lax.fori_loop(0, count, forward, 0)

    def backward(step, carry):
        c = count - 1 - step
        for h in all_heads:
            retreat(c, h)
        for h in all_heads:
            gradients(c, h)
        return carry

    lax.fori_loop(0, count, backward, 0)


def per_device(segment_input, views, gate_vec, base_rate, norm_gain, init_weight, out_grad):
    count = lax.axis_size("ctx")
    size, features = segment_input.shape[1:]
    total, width = gate_vec.shape[1:]
    heads = total // count
    local = heads * width

    def spread(value):
        parts = value[0].reshape(size, count, local).swapaxes(0, 1)
        return lax.all_to_all(parts, "ctx", 0, 0, tiled=True)

    def collect(value, steps):
        moved = lax.all_to_all(value, "ctx", 0, 0, tiled=True)
        number = lax.axis_size("segment")
        pairs = [(source, (source + steps) % number) for source in range(number)]
        moved = lax.ppermute(moved, "segment", pairs)
        return moved.swapaxes(0, 1).reshape(1, size, features)

    def shaped(shape, kind):
        return jax.ShapeDtypeStruct(shape, kind)

    vmem = pl.BlockSpec(memory_space=pltpu.VMEM)
    hbm = pl.BlockSpec(memory_space=pl.ANY)

    def pairs(rows, columns):
        return pltpu.VMEM((count, heads, 2, rows, columns), BF16)

    def floats(rows, columns):
        return pltpu.VMEM((count, heads, rows, columns), F32)

    result = pl.pallas_call(
        functools.partial(kernel, count, heads, size, width),
        out_shape=(
            shaped((count, size, local), BF16),
            shaped((1, heads, width, 3 * width), F32),
            shaped((1, heads, width), F32),
            shaped((1, heads), F32),
            shaped((1, heads, width), F32),
            shaped((1, heads, width, width), F32),
            shaped((count, size, local), BF16),
        ),
        in_specs=[vmem, vmem, hbm, vmem, vmem, vmem, hbm],
        out_specs=(vmem,) * 7,
        scratch_shapes=[
            pltpu.VMEM((heads, width, 3 * width), BF16),
            pltpu.VMEM((heads, width, width), F32),
            pairs(size, width), pairs(size, width), pairs(size, width), pairs(size, width), pairs(size, width),
            pairs(size, size), pairs(size, size), pairs(width, width),
            pairs(size, width), pairs(size, width), pairs(width, width), pairs(width, width),
            floats(size, width), floats(size, width), floats(size, width), floats(width, width),
            floats(size, width), floats(width, width),
            floats(size, 1), floats(size, 1),
            pltpu.SemaphoreType.DMA((2,)),
        ],
        compiler_params=pltpu.CompilerParams(vmem_limit_bytes=56 * 1024 * 1024),
    )(
        spread(segment_input), spread(out_grad), views, gate_vec, base_rate, norm_gain, init_weight
    )
    out, vgrad, ggrad, rgrad, ngrad, igrad, dx = result
    return (collect(out, 1), vgrad, ggrad, rgrad, ngrad, igrad, collect(dx, -1))


def solution(mesh):
    return jax.shard_map(
        per_device,
        mesh=mesh,
        in_specs=(
            P("segment", "ctx", None),
            P("segment", None, None, None),
            P("segment", None, None),
            P("segment", None),
            P("segment", None, None),
            P("segment", None, None, None),
            P("segment", "ctx", None),
        ),
        out_specs=(
            P("segment", "ctx", None),
            P("segment", "ctx", None, None),
            P("segment", "ctx", None),
            P("segment", "ctx"),
            P("segment", "ctx", None),
            P("segment", "ctx", None, None),
            P("segment", "ctx", None),
        ),
        check_vma=False,
    )
```

```python
import functools

import jax
import jax.numpy as jnp
from jax import lax
from jax.experimental import pallas as pl
from jax.experimental.pallas import tpu as pltpu
from jax.sharding import PartitionSpec as P

MB = 16
F32 = jnp.float32
BF16 = jnp.bfloat16
MESH = pl.DeviceIdType.MESH
NN = (((1,), (0,)), ((), ()))
NT = (((1,), (1,)), ((), ()))
TN = (((0,), (0,)), ((), ()))


def dot(left, right, dims):
    return lax.dot_general(left, right, dims, preferred_element_type=F32)


def split(value):
    high = value.astype(BF16)
    low = (value - high.astype(F32)).astype(BF16)
    return high, low


def cat(parts, axis):
    return jnp.concatenate(parts, axis=axis)


def stack(left, right, axis):
    return cat([left[0], right[0]], axis), cat([left[1], right[1]], axis)


def product(left, right, dims):
    left_axis, right_axis = dims[0][0][0], dims[0][1][0]
    left_both = cat(left, left_axis)
    wide = cat(right, 1 - right_axis)
    result = dot(left_both, cat([wide, wide], right_axis), dims)
    columns = result.shape[1] // 2
    return result[:, :columns] + result[:, columns:]


def row_mean(value):
    return jnp.mean(value, axis=-1, keepdims=True)


def positions(size):
    rows = lax.broadcasted_iota(jnp.int32, (size, size), 0)
    columns = lax.broadcasted_iota(jnp.int32, (size, size), 1)
    return rows, columns


def block_inverse(strict, size):
    rows, columns = positions(size)
    width = MB
    eye = jnp.where(rows == columns, 1.0, 0.0).astype(F32)
    inverse = eye
    while width < size:
        same = (rows // (2 * width)) == (columns // (2 * width))
        below = (rows // width) > (columns // width)
        corner = jnp.where(same & below, strict, 0.0)
        if width == MB:
            inverse = eye - corner
        else:
            pair = split(inverse)
            inverse = inverse - product(split(product(pair, split(corner), NN)), pair, NN)
        width *= 2
    return inverse


def kernel(
    count, sections, heads, size, width,
    x_ref, og_ref, views_ref, gate_ref, rate_ref, gain_ref, init_ref,
    next_ref, vgrad_ref, ggrad_ref, rgrad_ref, ngrad_ref, igrad_ref, prev_ref,
    view_buf, init_buf, x_buf, og_buf, out_buf, dx_buf,
    qs, ks, krs, qes, as_, ss, ts, fs, rs, dzs, ws,
    kf, bs, sbs, os_, v0s, ls, invs, sigs,
    load_sem, x_send, x_recv, og_send, og_recv, out_send, out_recv, dx_send, dx_recv,
):
    me = lax.axis_index("ctx")
    section = lax.axis_index("segment")
    after = (section + 1) % sections
    before_me = (section + sections - 1) % sections
    first_head = me * heads
    local = heads * width

    def partner(step):
        if count & (count - 1):
            return (me + step) % count
        total, bit = 0, 1
        while bit < count:
            total = total + (((me // bit) + (step // bit)) % 2) * bit
            bit *= 2
        return total

    def own_columns(owner):
        return pl.ds(pl.multiple_of(owner * local, local), local)

    loads = [
        pltpu.make_async_copy(views_ref.at[0, pl.ds(first_head, heads)], view_buf, load_sem.at[0]),
        pltpu.make_async_copy(init_ref.at[0, pl.ds(first_head, heads)], init_buf, load_sem.at[1]),
        pltpu.make_async_copy(x_ref.at[0, :, own_columns(me)], x_buf.at[me], x_recv.at[me]),
        pltpu.make_async_copy(og_ref.at[0, :, own_columns(me)], og_buf.at[me], og_recv.at[me]),
    ]
    for load in loads:
        load.start()

    barrier = pltpu.get_barrier_semaphore()
    for step in range(1, count):
        pl.semaphore_signal(barrier, inc=1, device_id=(section, partner(step)), device_id_type=MESH)
    for step in range(count):
        pl.semaphore_signal(barrier, inc=1, device_id=(after, partner(step)), device_id_type=MESH)
        pl.semaphore_signal(barrier, inc=1, device_id=(before_me, partner(step)), device_id_type=MESH)
    pl.semaphore_wait(barrier, 3 * count - 1)

    def spread(source, target, send, receive, step):
        owner = partner(step)
        return pltpu.make_async_remote_copy(
            src_ref=source.at[0, :, own_columns(owner)],
            dst_ref=target.at[me],
            send_sem=send.at[step],
            recv_sem=receive.at[me],
            device_id=(section, owner),
            device_id_type=MESH,
        )

    def arrived(target, receive, c):
        pltpu.make_async_copy(target.at[c], target.at[c], receive.at[c]).wait()

    def collect(source, target, send, receive, c, to):
        return pltpu.make_async_remote_copy(
            src_ref=source.at[c],
            dst_ref=target.at[0, :, own_columns(me)],
            send_sem=send.at[c],
            recv_sem=receive.at[me],
            device_id=(to, c),
            device_id_type=MESH,
        )

    def collected(target, receive, c):
        place = target.at[0, :, own_columns(c)]
        pltpu.make_async_copy(place, place, receive.at[c]).wait()

    for step in range(1, count):
        spread(x_ref, x_buf, x_send, x_recv, step).start()
    for load in loads[:2]:
        load.wait()
    scale = 1.0 / (MB * width)

    def columns_of(h):
        return slice(h * width, (h + 1) * width)

    def gate_of(h):
        return gate_ref[0, pl.ds(first_head + h, 1), :]

    def gain_of(h):
        return gain_ref[0, pl.ds(first_head + h, 1), :]

    def base_of(h):
        lane = lax.broadcasted_iota(jnp.int32, rate_ref.shape, 1)
        return jnp.sum(jnp.where(lane == first_head + h, rate_ref[...], 0.0), axis=1, keepdims=True)

    def put(ref, c, h, pair):
        ref[c, h, 0] = pair[0]
        ref[c, h, 1] = pair[1]

    def get(ref, c, h):
        return ref[c, h, 0], ref[c, h, 1]

    def masks():
        rows, columns = positions(size)
        return rows >= columns, (rows // MB) > (columns // MB)

    def prepare(c, h):
        x = x_buf[c, :, columns_of(h)]
        packed = dot(x, view_buf[h], NN)
        q = packed[:, :width]
        raw = packed[:, width : 2 * width]
        inv = lax.rsqrt(row_mean(raw * raw) + 1e-06)
        k = raw * inv
        y = packed[:, 2 * width :] - k
        logit = jnp.sum(x.astype(F32) * gate_of(h), axis=-1, keepdims=True)
        sig = jax.nn.sigmoid(logit)
        kr = k * (base_of(h) * sig * scale)
        k2, q2, kr2 = split(k), split(q), split(kr)
        causal, before = masks()
        grams = product(stack(k2, q2, 0), kr2, NT)
        inverse = block_inverse(jnp.where(before, grams[:size], 0.0), size)
        scores = split(jnp.where(causal, grams[size:], 0.0))
        t2 = split(inverse)
        ab = product(t2, stack(k2, split(y), 1), NN)
        ab2 = split(ab)
        sab = product(scores, ab2, NN)
        fo = product(kr2, ab2, TN)
        put(qs, c, h, q2)
        put(ks, c, h, k2)
        put(krs, c, h, kr2)
        put(qes, c, h, split(q - sab[:, :width]))
        put(as_, c, h, (ab2[0][:, :width], ab2[1][:, :width]))
        put(ss, c, h, scores)
        put(ts, c, h, t2)
        put(fs, c, h, split(fo[:, :width]))
        kf[c, h] = k
        bs[c, h] = ab[:, width:]
        sbs[c, h] = sab[:, width:]
        os_[c, h] = fo[:, width:]
        invs[c, h] = inv
        sigs[c, h] = sig

    def advance(c, h, w2):
        init_buf[h] = init_buf[h] - product(get(fs, c, h), w2, NN) + os_[c, h]

    def outputs(c, h, w2):
        cols = columns_of(h)
        qe = get(qes, c, h)
        moved = product(stack(qe, get(as_, c, h), 0), w2, NN)
        z = moved[:size] + sbs[c, h]
        put(rs, c, h, split(moved[size:] - bs[c, h]))
        centred = z - row_mean(z)
        rstd = lax.rsqrt(row_mean(centred * centred) + 1e-05)
        normed = centred * rstd
        gain = gain_of(h)
        out_buf[c, :, cols] = (x_buf[c, :, cols].astype(F32) + gain * normed).astype(BF16)
        dout = og_buf[c, :, cols].astype(F32)
        ngrad_ref[0, h : h + 1, :] += jnp.sum(dout * normed, axis=0, keepdims=True)
        dn = dout * gain
        dz = rstd * (dn - row_mean(dn) - normed * row_mean(dn * normed))
        dz2 = split(dz)
        put(dzs, c, h, dz2)
        back = product(stack(qe, get(ss, c, h), 1), dz2, TN)
        ls[c, h] = back[:width]
        v0s[c, h] = back[width:]

    def retreat(c, h, g2):
        igrad_ref[0, h] = igrad_ref[0, h] - product(get(fs, c, h), g2, TN) + ls[c, h]

    def gradients(c, h, g2):
        cols = columns_of(h)
        kr2, w2, r2, dz2 = get(krs, c, h), get(ws, c, h), get(rs, c, h), get(dzs, c, h)
        v = v0s[c, h] + product(kr2, g2, NN)
        du = -product(get(ts, c, h), split(v), TN)
        both = stack(dz2, split(du), 0)
        causal, before = masks()
        inner = product(both, r2, NT)
        dscores = jnp.where(causal, -inner[:size], 0.0)
        dstrict = jnp.where(before, -inner[size:], 0.0)
        d2 = stack(split(dscores), split(dstrict), 0)
        dqk = product(both, w2, NT) + product(d2, kr2, NN)
        dkr = product(d2, stack(get(qs, c, h), get(ks, c, h), 0), TN) - product(r2, g2, NT)
        sig, inv, k, base = sigs[c, h], invs[c, h], kf[c, h], base_of(h)
        rate_factor = sig * scale
        dk = dqk[size:] + (base * rate_factor) * dkr + du
        draw = inv * (dk - k * row_mean(dk * k))
        drate = jnp.sum(dkr * k, axis=-1, keepdims=True) * rate_factor
        rgrad_ref[:, h : h + 1] += jnp.sum(drate, axis=0, keepdims=True)
        dlogit = drate * base * (1.0 - sig)
        x = x_buf[c, :, cols]
        ggrad_ref[0, h : h + 1, :] += jnp.sum(dlogit * x.astype(F32), axis=0, keepdims=True)
        packed = split(cat([dqk[:size], draw, -du], 1))
        vgrad_ref[0, h] += dot(cat([x, x], 0), cat(packed, 0), TN)
        views = view_buf[h]
        dx = dot(packed[0], views, NT) + dot(packed[1], views, NT)
        dx = dx + og_buf[c, :, cols].astype(F32) + dlogit * gate_of(h)
        dx_buf[c, :, cols] = dx.astype(BF16)

    for ref in (vgrad_ref, ggrad_ref, rgrad_ref, ngrad_ref, igrad_ref):
        ref[...] = jnp.zeros_like(ref)

    all_heads = range(heads)

    def prepare_step(step, carry):
        c = partner(step)
        arrived(x_buf, x_recv, c)
        for h in all_heads:
            prepare(c, h)
        return carry

    half = count // 2
    lax.fori_loop(0, half, prepare_step, 0)
    for step in range(1, count):
        spread(og_ref, og_buf, og_send, og_recv, step).start()
    lax.fori_loop(half, count, prepare_step, 0)

    def forward(c, carry):
        arrived(og_buf, og_recv, c)
        starts = [split(init_buf[h]) for h in all_heads]
        for h in all_heads:
            put(ws, c, h, starts[h])
            advance(c, h, starts[h])
        for h in all_heads:
            outputs(c, h, starts[h])
        collect(out_buf, next_ref, out_send, out_recv, c, after).start()
        return carry

    lax.fori_loop(0, count, forward, 0)

    def backward(step, carry):
        c = count - 1 - step
        ends = [split(igrad_ref[0, h]) for h in all_heads]
        for h in all_heads:
            retreat(c, h, ends[h])
        for h in all_heads:
            gradients(c, h, ends[h])
        collect(dx_buf, prev_ref, dx_send, dx_recv, c, before_me).start()
        return carry

    lax.fori_loop(0, count, backward, 0)

    for step in range(1, count):
        spread(x_ref, x_buf, x_send, x_recv, step).wait_send()
        spread(og_ref, og_buf, og_send, og_recv, step).wait_send()
    for c in range(count):
        collect(out_buf, next_ref, out_send, out_recv, c, after).wait_send()
        collect(dx_buf, prev_ref, dx_send, dx_recv, c, before_me).wait_send()
        collected(next_ref, out_recv, c)
        collected(prev_ref, dx_recv, c)


def per_device(segment_input, views, gate_vec, base_rate, norm_gain, init_weight, out_grad):
    count = lax.axis_size("ctx")
    size, features = segment_input.shape[1:]
    total, width = gate_vec.shape[1:]
    heads = total // count
    local = heads * width

    def shaped(shape, kind):
        return jax.ShapeDtypeStruct(shape, kind)

    vmem = pl.BlockSpec(memory_space=pltpu.VMEM)
    hbm = pl.BlockSpec(memory_space=pl.ANY)

    chunks = pltpu.VMEM((count, size, local), BF16)

    def pairs(rows, columns):
        return pltpu.VMEM((count, heads, 2, rows, columns), BF16)

    def floats(rows, columns):
        return pltpu.VMEM((count, heads, rows, columns), F32)

    return pl.pallas_call(
        functools.partial(kernel, count, lax.axis_size("segment"), heads, size, width),
        out_shape=(
            shaped((1, size, features), BF16),
            shaped((1, heads, width, 3 * width), F32),
            shaped((1, heads, width), F32),
            shaped((1, heads), F32),
            shaped((1, heads, width), F32),
            shaped((1, heads, width, width), F32),
            shaped((1, size, features), BF16),
        ),
        in_specs=[hbm, hbm, hbm, vmem, vmem, vmem, hbm],
        out_specs=(hbm,) + (vmem,) * 5 + (hbm,),
        scratch_shapes=[
            pltpu.VMEM((heads, width, 3 * width), BF16),
            pltpu.VMEM((heads, width, width), F32),
            chunks, chunks, chunks, chunks,
            pairs(size, width), pairs(size, width), pairs(size, width), pairs(size, width), pairs(size, width),
            pairs(size, size), pairs(size, size), pairs(width, width),
            pairs(size, width), pairs(size, width), pairs(width, width),
            floats(size, width), floats(size, width), floats(size, width), floats(width, width),
            floats(size, width), floats(width, width),
            floats(size, 1), floats(size, 1),
            pltpu.SemaphoreType.DMA((2,)),
            *[pltpu.SemaphoreType.DMA((count,))] * 8,
        ],
        compiler_params=pltpu.CompilerParams(
            vmem_limit_bytes=56 * 1024 * 1024, collective_id=0, has_side_effects=True
        ),
    )(
        segment_input, out_grad, views, gate_vec, base_rate, norm_gain, init_weight
    )


def solution(mesh):
    return jax.shard_map(
        per_device,
        mesh=mesh,
        in_specs=(
            P("segment", "ctx", None),
            P("segment", None, None, None),
            P("segment", None, None),
            P("segment", None),
            P("segment", None, None),
            P("segment", None, None, None),
            P("segment", "ctx", None),
        ),
        out_specs=(
            P("segment", "ctx", None),
            P("segment", "ctx", None, None),
            P("segment", "ctx", None),
            P("segment", "ctx"),
            P("segment", "ctx", None),
            P("segment", "ctx", None, None),
            P("segment", "ctx", None),
        ),
        check_vma=False,
    )
```

```python
import functools

import jax
import jax.numpy as jnp
from jax import lax
from jax.experimental import pallas as pl
from jax.experimental.pallas import tpu as pltpu
from jax.sharding import PartitionSpec as P

MB = 16
F32 = jnp.float32
BF16 = jnp.bfloat16
MESH = pl.DeviceIdType.MESH
NN = (((1,), (0,)), ((), ()))
NT = (((1,), (1,)), ((), ()))
TN = (((0,), (0,)), ((), ()))


def dot(left, right, dims):
    return lax.dot_general(left, right, dims, preferred_element_type=F32)


def split(value):
    high = value.astype(BF16)
    low = (value - high.astype(F32)).astype(BF16)
    return high, low


def cat(parts, axis):
    return jnp.concatenate(parts, axis=axis)


def stack(left, right, axis):
    return cat([left[0], right[0]], axis), cat([left[1], right[1]], axis)


def product(left, right, dims):
    left_axis, right_axis = dims[0][0][0], dims[0][1][0]
    left_both = cat(left, left_axis)
    wide = cat(right, 1 - right_axis)
    result = dot(left_both, cat([wide, wide], right_axis), dims)
    columns = result.shape[1] // 2
    return result[:, :columns] + result[:, columns:]


def row_mean(value):
    return jnp.mean(value, axis=-1, keepdims=True)


def fill_masks(ref, size):
    rows = lax.broadcasted_iota(jnp.int32, (size, size), 0)
    columns = lax.broadcasted_iota(jnp.int32, (size, size), 1)
    chosen = [rows >= columns, (rows // MB) > (columns // MB), rows == columns]
    block = MB
    while block < size:
        same = (rows // (2 * block)) == (columns // (2 * block))
        chosen.append(same & ((rows // block) > (columns // block)))
        block *= 2
    for index, mask in enumerate(chosen):
        ref[index] = jnp.where(mask, 1.0, 0.0).astype(F32)


def levels_of(size):
    levels, block = 0, MB
    while block < size:
        levels, block = levels + 1, 2 * block
    return levels


def together(streams):
    streams = list(streams)
    while streams:
        alive = []
        for stream in streams:
            try:
                next(stream)
                alive.append(stream)
            except StopIteration:
                pass
        streams = alive


def kernel(
    count, sections, heads, size, width,
    x_ref, og_ref, views_ref, gate_ref, rate_ref, gain_ref, init_ref,
    next_ref, vgrad_ref, ggrad_ref, rgrad_ref, ngrad_ref, igrad_ref, prev_ref,
    view_buf, init_buf, x_buf, og_buf, out_buf, dx_buf, masks,
    qs, ks, krs, qes, as_, ss, ts, fs, rs, dzs, ws,
    kf, bs, sbs, os_, v0s, ls, invs, sigs,
    load_sem, x_send, x_recv, og_send, og_recv, out_send, out_recv, dx_send, dx_recv,
):
    me = lax.axis_index("ctx")
    section = lax.axis_index("segment")
    after = (section + 1) % sections
    before_me = (section + sections - 1) % sections
    first_head = me * heads
    local = heads * width

    def partner(step):
        if count & (count - 1):
            return (me + step) % count
        total, bit = 0, 1
        while bit < count:
            total = total + (((me // bit) + (step // bit)) % 2) * bit
            bit *= 2
        return total

    def own_columns(owner):
        return pl.ds(pl.multiple_of(owner * local, local), local)

    loads = [
        pltpu.make_async_copy(views_ref.at[0, pl.ds(first_head, heads)], view_buf, load_sem.at[0]),
        pltpu.make_async_copy(init_ref.at[0, pl.ds(first_head, heads)], init_buf, load_sem.at[1]),
        pltpu.make_async_copy(x_ref.at[0, :, own_columns(me)], x_buf.at[me], x_recv.at[me]),
        pltpu.make_async_copy(og_ref.at[0, :, own_columns(me)], og_buf.at[me], og_recv.at[me]),
    ]
    for load in loads:
        load.start()

    barrier = pltpu.get_barrier_semaphore()
    for step in range(1, count):
        pl.semaphore_signal(barrier, inc=1, device_id=(section, partner(step)), device_id_type=MESH)
    for step in range(count):
        pl.semaphore_signal(barrier, inc=1, device_id=(after, partner(step)), device_id_type=MESH)
        pl.semaphore_signal(barrier, inc=1, device_id=(before_me, partner(step)), device_id_type=MESH)
    pl.semaphore_wait(barrier, 3 * count - 1)

    def spread(source, target, send, receive, step):
        owner = partner(step)
        return pltpu.make_async_remote_copy(
            src_ref=source.at[0, :, own_columns(owner)],
            dst_ref=target.at[me],
            send_sem=send.at[step],
            recv_sem=receive.at[me],
            device_id=(section, owner),
            device_id_type=MESH,
        )

    def arrived(target, receive, c):
        pltpu.make_async_copy(target.at[c], target.at[c], receive.at[c]).wait()

    def collect(source, target, send, receive, c, to):
        return pltpu.make_async_remote_copy(
            src_ref=source.at[c],
            dst_ref=target.at[0, :, own_columns(me)],
            send_sem=send.at[c],
            recv_sem=receive.at[me],
            device_id=(to, c),
            device_id_type=MESH,
        )

    def collected(target, receive, c):
        place = target.at[0, :, own_columns(c)]
        pltpu.make_async_copy(place, place, receive.at[c]).wait()

    for step in range(1, count):
        spread(x_ref, x_buf, x_send, x_recv, step).start()
    for load in loads[:2]:
        load.wait()
    scale = 1.0 / (MB * width)
    levels = levels_of(size)
    fill_masks(masks, size)

    def columns_of(h):
        return slice(h * width, (h + 1) * width)

    def gate_of(h):
        return gate_ref[0, pl.ds(first_head + h, 1), :]

    def gain_of(h):
        return gain_ref[0, pl.ds(first_head + h, 1), :]

    def base_of(h):
        lane = lax.broadcasted_iota(jnp.int32, rate_ref.shape, 1)
        return jnp.sum(jnp.where(lane == first_head + h, rate_ref[...], 0.0), axis=1, keepdims=True)

    def put(ref, c, h, pair):
        ref[c, h, 0] = pair[0]
        ref[c, h, 1] = pair[1]

    def get(ref, c, h):
        return ref[c, h, 0], ref[c, h, 1]

    def prepare(c, h):
        x = x_buf[c, :, columns_of(h)]
        packed = dot(x, view_buf[h], NN)
        yield
        q = packed[:, :width]
        raw = packed[:, width : 2 * width]
        inv = lax.rsqrt(row_mean(raw * raw) + 1e-06)
        k = raw * inv
        y = packed[:, 2 * width :] - k
        logit = jnp.sum(x.astype(F32) * gate_of(h), axis=-1, keepdims=True)
        sig = jax.nn.sigmoid(logit)
        kr = k * (base_of(h) * sig * scale)
        k2, q2, kr2 = split(k), split(q), split(kr)
        y2 = split(y)
        yield
        grams = product(stack(k2, q2, 0), kr2, NT)
        yield
        scores = split(masks[0] * grams[size:])
        strict = grams[:size]
        inverse = masks[2] - masks[3] * strict if levels else masks[2]
        t2 = split(inverse)
        for level in range(1, levels):
            half_way = product(t2, split(masks[3 + level] * strict), NN)
            yield
            inverse = inverse - product(split(half_way), t2, NN)
            t2 = split(inverse)
            yield
        ab = product(t2, stack(k2, y2, 1), NN)
        yield
        ab2 = split(ab)
        sab = product(scores, ab2, NN)
        fo = product(kr2, ab2, TN)
        yield
        put(qs, c, h, q2)
        put(ks, c, h, k2)
        put(krs, c, h, kr2)
        put(qes, c, h, split(q - sab[:, :width]))
        put(as_, c, h, (ab2[0][:, :width], ab2[1][:, :width]))
        put(ss, c, h, scores)
        put(ts, c, h, t2)
        put(fs, c, h, split(fo[:, :width]))
        kf[c, h] = k
        bs[c, h] = ab[:, width:]
        sbs[c, h] = sab[:, width:]
        os_[c, h] = fo[:, width:]
        invs[c, h] = inv
        sigs[c, h] = sig

    def outputs(c, h, w2):
        cols = columns_of(h)
        qe = get(qes, c, h)
        moved = product(stack(qe, get(as_, c, h), 0), w2, NN)
        yield
        z = moved[:size] + sbs[c, h]
        put(rs, c, h, split(moved[size:] - bs[c, h]))
        centred = z - row_mean(z)
        yield
        rstd = lax.rsqrt(row_mean(centred * centred) + 1e-05)
        normed = centred * rstd
        gain = gain_of(h)
        out_buf[c, :, cols] = (x_buf[c, :, cols].astype(F32) + gain * normed).astype(BF16)
        dout = og_buf[c, :, cols].astype(F32)
        ngrad_ref[0, h : h + 1, :] += jnp.sum(dout * normed, axis=0, keepdims=True)
        dn = dout * gain
        dz = rstd * (dn - row_mean(dn) - normed * row_mean(dn * normed))
        dz2 = split(dz)
        put(dzs, c, h, dz2)
        yield
        back = product(stack(qe, get(ss, c, h), 1), dz2, TN)
        yield
        ls[c, h] = back[:width]
        v0s[c, h] = back[width:]

    def gradients(c, h, g2):
        cols = columns_of(h)
        kr2, w2, r2, dz2 = get(krs, c, h), get(ws, c, h), get(rs, c, h), get(dzs, c, h)
        v = v0s[c, h] + product(kr2, g2, NN)
        yield
        du = -product(get(ts, c, h), split(v), TN)
        yield
        both = stack(dz2, split(du), 0)
        inner = product(both, r2, NT)
        yield
        d2 = stack(split(-masks[0] * inner[:size]), split(-masks[1] * inner[size:]), 0)
        dqk = product(both, w2, NT) + product(d2, kr2, NN)
        yield
        dkr = product(d2, stack(get(qs, c, h), get(ks, c, h), 0), TN) - product(r2, g2, NT)
        yield
        sig, inv, k, base = sigs[c, h], invs[c, h], kf[c, h], base_of(h)
        rate_factor = sig * scale
        dk = dqk[size:] + (base * rate_factor) * dkr + du
        draw = inv * (dk - k * row_mean(dk * k))
        drate = jnp.sum(dkr * k, axis=-1, keepdims=True) * rate_factor
        rgrad_ref[:, h : h + 1] += jnp.sum(drate, axis=0, keepdims=True)
        dlogit = drate * base * (1.0 - sig)
        x = x_buf[c, :, cols]
        ggrad_ref[0, h : h + 1, :] += jnp.sum(dlogit * x.astype(F32), axis=0, keepdims=True)
        packed = split(cat([dqk[:size], draw, -du], 1))
        yield
        vgrad_ref[0, h] += dot(cat([x, x], 0), cat(packed, 0), TN)
        views = view_buf[h]
        dx = dot(packed[0], views, NT) + dot(packed[1], views, NT)
        dx = dx + og_buf[c, :, cols].astype(F32) + dlogit * gate_of(h)
        dx_buf[c, :, cols] = dx.astype(BF16)

    for ref in (vgrad_ref, ggrad_ref, rgrad_ref, ngrad_ref, igrad_ref):
        ref[...] = jnp.zeros_like(ref)

    all_heads = range(heads)

    pairing = 2 if count % 4 == 0 else 1
    by = range(pairing)

    def prepare_step(step, carry):
        chunks = [partner(step * pairing + i) for i in by]
        for c in chunks:
            arrived(x_buf, x_recv, c)
        together(prepare(c, h) for c in chunks for h in all_heads)
        return carry

    rounds = count // pairing
    half = rounds // 2
    lax.fori_loop(0, half, prepare_step, 0)
    for step in range(1, count):
        spread(og_ref, og_buf, og_send, og_recv, step).start()
    lax.fori_loop(half, rounds, prepare_step, 0)

    def forward_stream(c, h, w, ends):
        w2 = split(w)
        put(ws, c, h, w2)
        ends[h] = w - product(get(fs, c, h), w2, NN) + os_[c, h]
        yield
        yield from outputs(c, h, w2)

    def forward(step, carry):
        chunks = [step * pairing + i for i in by]
        for c in chunks:
            arrived(og_buf, og_recv, c)
        now = {h: init_buf[h] for h in all_heads}
        streams = []
        for c in chunks:
            ends = {}
            fresh = [forward_stream(c, h, now[h], ends) for h in all_heads]
            for stream in fresh:
                next(stream)
            streams += fresh
            now = ends
        for h in all_heads:
            init_buf[h] = now[h]
        together(streams)
        for c in chunks:
            collect(out_buf, next_ref, out_send, out_recv, c, after).start()
        return carry

    lax.fori_loop(0, rounds, forward, 0)

    def backward_stream(c, h, g, starts):
        g2 = split(g)
        starts[h] = g - product(get(fs, c, h), g2, TN) + ls[c, h]
        yield
        yield from gradients(c, h, g2)

    def backward(step, carry):
        chunks = [count - 1 - (step * pairing + i) for i in by]
        now = {h: igrad_ref[0, h] for h in all_heads}
        streams = []
        for c in chunks:
            starts = {}
            fresh = [backward_stream(c, h, now[h], starts) for h in all_heads]
            for stream in fresh:
                next(stream)
            streams += fresh
            now = starts
        for h in all_heads:
            igrad_ref[0, h] = now[h]
        together(streams)
        for c in chunks:
            collect(dx_buf, prev_ref, dx_send, dx_recv, c, before_me).start()
        return carry

    lax.fori_loop(0, rounds, backward, 0)

    for step in range(1, count):
        spread(x_ref, x_buf, x_send, x_recv, step).wait_send()
        spread(og_ref, og_buf, og_send, og_recv, step).wait_send()
    for c in range(count):
        collect(out_buf, next_ref, out_send, out_recv, c, after).wait_send()
        collect(dx_buf, prev_ref, dx_send, dx_recv, c, before_me).wait_send()
        collected(next_ref, out_recv, c)
        collected(prev_ref, dx_recv, c)


def hand_over(*refs):
    number = (len(refs) - 1) // 2
    copies = [pltpu.make_async_copy(refs[i], refs[number + i], refs[-1].at[i]) for i in range(number)]
    for copy in copies:
        copy.start()
    for copy in copies:
        copy.wait()


def per_device(segment_input, views, gate_vec, base_rate, norm_gain, init_weight, out_grad):
    count = lax.axis_size("ctx")
    size, features = segment_input.shape[1:]
    total, width = gate_vec.shape[1:]
    heads = total // count
    local = heads * width

    def shaped(shape, kind):
        return jax.ShapeDtypeStruct(shape, kind)

    vmem = pl.BlockSpec(memory_space=pltpu.VMEM)
    hbm = pl.BlockSpec(memory_space=pl.ANY)

    chunks = pltpu.VMEM((count, size, local), BF16)

    def pairs(rows, columns):
        return pltpu.VMEM((count, heads, 2, rows, columns), BF16)

    def floats(rows, columns):
        return pltpu.VMEM((count, heads, rows, columns), F32)

    results = pl.pallas_call(
        functools.partial(kernel, count, lax.axis_size("segment"), heads, size, width),
        out_shape=(
            shaped((1, size, features), BF16),
            shaped((1, heads, width, 3 * width), F32),
            shaped((1, heads, width), F32),
            shaped((1, heads), F32),
            shaped((1, heads, width), F32),
            shaped((1, heads, width, width), F32),
            shaped((1, size, features), BF16),
        ),
        in_specs=[hbm, hbm, hbm, vmem, vmem, vmem, hbm],
        out_specs=(hbm,) + (vmem,) * 5 + (hbm,),
        scratch_shapes=[
            pltpu.VMEM((heads, width, 3 * width), BF16),
            pltpu.VMEM((heads, width, width), F32),
            chunks, chunks, chunks, chunks,
            pltpu.VMEM((3 + levels_of(size), size, size), F32),
            pairs(size, width), pairs(size, width), pairs(size, width), pairs(size, width), pairs(size, width),
            pairs(size, size), pairs(size, size), pairs(width, width),
            pairs(size, width), pairs(size, width), pairs(width, width),
            floats(size, width), floats(size, width), floats(size, width), floats(width, width),
            floats(size, width), floats(width, width),
            floats(size, 1), floats(size, 1),
            pltpu.SemaphoreType.DMA((2,)),
            *[pltpu.SemaphoreType.DMA((count,))] * 8,
        ],
        compiler_params=pltpu.CompilerParams(
            vmem_limit_bytes=56 * 1024 * 1024, collective_id=0, has_side_effects=True
        ),
    )(
        segment_input, out_grad, views, gate_vec, base_rate, norm_gain, init_weight
    )
    return pl.pallas_call(
        hand_over,
        out_shape=tuple(shaped(value.shape, value.dtype) for value in results),
        in_specs=[hbm] * len(results),
        out_specs=(vmem,) * len(results),
        scratch_shapes=[pltpu.SemaphoreType.DMA((len(results),))],
    )(*results)


def solution(mesh):
    return jax.shard_map(
        per_device,
        mesh=mesh,
        in_specs=(
            P("segment", "ctx", None),
            P("segment", None, None, None),
            P("segment", None, None),
            P("segment", None),
            P("segment", None, None),
            P("segment", None, None, None),
            P("segment", "ctx", None),
        ),
        out_specs=(
            P("segment", "ctx", None),
            P("segment", "ctx", None, None),
            P("segment", "ctx", None),
            P("segment", "ctx"),
            P("segment", "ctx", None),
            P("segment", "ctx", None, None),
            P("segment", "ctx", None),
        ),
        check_vma=False,
    )
```

```python
import functools

import jax
import jax.numpy as jnp
from jax import lax
from jax.experimental import pallas as pl
from jax.experimental.pallas import tpu as pltpu
from jax.sharding import PartitionSpec as P

MB = 16
F32 = jnp.float32
BF16 = jnp.bfloat16
MESH = pl.DeviceIdType.MESH
NN = (((1,), (0,)), ((), ()))
NT = (((1,), (1,)), ((), ()))
TN = (((0,), (0,)), ((), ()))


def dot(left, right, dims):
    return lax.dot_general(left, right, dims, preferred_element_type=F32)


def split(value):
    high = value.astype(BF16)
    low = (value - high.astype(F32)).astype(BF16)
    return high, low


def cat(parts, axis):
    return jnp.concatenate(parts, axis=axis)


def stack(left, right, axis):
    return cat([left[0], right[0]], axis), cat([left[1], right[1]], axis)


def product(left, right, dims):
    left_axis, right_axis = dims[0][0][0], dims[0][1][0]
    left_both = cat(left, left_axis)
    wide = cat(right, 1 - right_axis)
    result = dot(left_both, cat([wide, wide], right_axis), dims)
    columns = result.shape[1] // 2
    return result[:, :columns] + result[:, columns:]


def row_mean(value):
    return jnp.mean(value, axis=-1, keepdims=True)


def fill_masks(ref, size):
    rows = lax.broadcasted_iota(jnp.int32, (size, size), 0)
    columns = lax.broadcasted_iota(jnp.int32, (size, size), 1)
    chosen = [rows >= columns, (rows // MB) > (columns // MB), rows == columns]
    block = MB
    while block < size:
        same = (rows // (2 * block)) == (columns // (2 * block))
        chosen.append(same & ((rows // block) > (columns // block)))
        block *= 2
    for index, mask in enumerate(chosen):
        ref[index] = jnp.where(mask, 1.0, 0.0).astype(F32)


def levels_of(size):
    levels, block = 0, MB
    while block < size:
        levels, block = levels + 1, 2 * block
    return levels


def together(streams):
    streams = list(streams)
    while streams:
        alive = []
        for stream in streams:
            try:
                next(stream)
                alive.append(stream)
            except StopIteration:
                pass
        streams = alive


def kernel(
    count, sections, heads, size, width,
    x_ref, og_ref, views_ref, gate_ref, rate_ref, gain_ref, init_ref,
    next_ref, vgrad_ref, ggrad_ref, rgrad_ref, ngrad_ref, igrad_ref, prev_ref,
    view_buf, init_buf, x_buf, og_buf, out_buf, dx_buf, masks,
    qs, ks, krs, qes, as_, ss, ts, fs, rs, dzs, ws, gs,
    kf, bs, sbs, os_, v0s, ls, ns, invs, sigs, rstds,
    load_sem, x_send, x_recv, og_send, og_recv, out_send, out_recv, dx_send, dx_recv,
):
    me = lax.axis_index("ctx")
    section = lax.axis_index("segment")
    after = (section + 1) % sections
    before_me = (section + sections - 1) % sections
    first_head = me * heads
    local = heads * width

    def partner(step):
        if count & (count - 1):
            return (me + step) % count
        total, bit = 0, 1
        while bit < count:
            total = total + (((me // bit) + (step // bit)) % 2) * bit
            bit *= 2
        return total

    def turn(step):
        if count % 2:
            return partner(step)
        return partner((step % 2) * (count // 2) + step // 2)

    def own_columns(owner):
        return pl.ds(pl.multiple_of(owner * local, local), local)

    loads = [
        pltpu.make_async_copy(views_ref.at[0, pl.ds(first_head, heads)], view_buf, load_sem.at[0]),
        pltpu.make_async_copy(init_ref.at[0, pl.ds(first_head, heads)], init_buf, load_sem.at[1]),
        pltpu.make_async_copy(x_ref.at[0, :, own_columns(me)], x_buf.at[me], x_recv.at[me]),
        pltpu.make_async_copy(og_ref.at[0, :, own_columns(me)], og_buf.at[me], og_recv.at[me]),
    ]
    for load in loads:
        load.start()

    barrier = pltpu.get_barrier_semaphore()
    for step in range(1, count):
        pl.semaphore_signal(barrier, inc=1, device_id=(section, partner(step)), device_id_type=MESH)
    for step in range(count):
        pl.semaphore_signal(barrier, inc=1, device_id=(after, partner(step)), device_id_type=MESH)
        pl.semaphore_signal(barrier, inc=1, device_id=(before_me, partner(step)), device_id_type=MESH)
    pl.semaphore_wait(barrier, 3 * count - 1)

    def spread(source, target, send, receive, step):
        owner = turn(step)
        return pltpu.make_async_remote_copy(
            src_ref=source.at[0, :, own_columns(owner)],
            dst_ref=target.at[me],
            send_sem=send.at[step],
            recv_sem=receive.at[me],
            device_id=(section, owner),
            device_id_type=MESH,
        )

    def arrived(target, receive, c):
        pltpu.make_async_copy(target.at[c], target.at[c], receive.at[c]).wait()

    def collect(source, target, send, receive, c, to):
        return pltpu.make_async_remote_copy(
            src_ref=source.at[c],
            dst_ref=target.at[0, :, own_columns(me)],
            send_sem=send.at[c],
            recv_sem=receive.at[me],
            device_id=(to, c),
            device_id_type=MESH,
        )

    def collected(target, receive, c):
        place = target.at[0, :, own_columns(c)]
        pltpu.make_async_copy(place, place, receive.at[c]).wait()

    for step in range(1, count):
        spread(x_ref, x_buf, x_send, x_recv, step).start()
    for load in loads[:2]:
        load.wait()
    scale = 1.0 / (MB * width)
    levels = levels_of(size)
    fill_masks(masks, size)

    def columns_of(h):
        return slice(h * width, (h + 1) * width)

    def gate_of(h):
        return gate_ref[0, pl.ds(first_head + h, 1), :]

    def gain_of(h):
        return gain_ref[0, pl.ds(first_head + h, 1), :]

    def base_of(h):
        lane = lax.broadcasted_iota(jnp.int32, rate_ref.shape, 1)
        return jnp.sum(jnp.where(lane == first_head + h, rate_ref[...], 0.0), axis=1, keepdims=True)

    def put(ref, c, h, pair):
        ref[c, h, 0] = pair[0]
        ref[c, h, 1] = pair[1]

    def get(ref, c, h):
        return ref[c, h, 0], ref[c, h, 1]

    def prepare(c, h):
        x = x_buf[c, :, columns_of(h)]
        packed = dot(x, view_buf[h], NN)
        yield
        q = packed[:, :width]
        raw = packed[:, width : 2 * width]
        inv = lax.rsqrt(row_mean(raw * raw) + 1e-06)
        k = raw * inv
        y = packed[:, 2 * width :] - k
        logit = jnp.sum(x.astype(F32) * gate_of(h), axis=-1, keepdims=True)
        sig = jax.nn.sigmoid(logit)
        kr = k * (base_of(h) * sig * scale)
        k2, q2, kr2 = split(k), split(q), split(kr)
        y2 = split(y)
        yield
        grams = product(stack(k2, q2, 0), kr2, NT)
        yield
        scores = split(masks[0] * grams[size:])
        strict = grams[:size]
        inverse = masks[2] - masks[3] * strict if levels else masks[2]
        t2 = split(inverse)
        for level in range(1, levels):
            half_way = product(t2, split(masks[3 + level] * strict), NN)
            yield
            inverse = inverse - product(split(half_way), t2, NN)
            t2 = split(inverse)
            yield
        ab = product(t2, stack(k2, y2, 1), NN)
        yield
        ab2 = split(ab)
        sab = product(scores, ab2, NN)
        fo = product(kr2, ab2, TN)
        yield
        put(qs, c, h, q2)
        put(ks, c, h, k2)
        put(krs, c, h, kr2)
        put(qes, c, h, split(q - sab[:, :width]))
        put(as_, c, h, (ab2[0][:, :width], ab2[1][:, :width]))
        put(ss, c, h, scores)
        put(ts, c, h, t2)
        put(fs, c, h, split(fo[:, :width]))
        kf[c, h] = k
        bs[c, h] = ab[:, width:]
        sbs[c, h] = sab[:, width:]
        os_[c, h] = fo[:, width:]
        invs[c, h] = inv
        sigs[c, h] = sig

    def emit(c, h):
        cols = columns_of(h)
        moved = product(stack(get(qes, c, h), get(as_, c, h), 0), get(ws, c, h), NN)
        yield
        z = moved[:size] + sbs[c, h]
        put(rs, c, h, split(moved[size:] - bs[c, h]))
        centred = z - row_mean(z)
        yield
        rstd = lax.rsqrt(row_mean(centred * centred) + 1e-05)
        normed = centred * rstd
        out_buf[c, :, cols] = (x_buf[c, :, cols].astype(F32) + gain_of(h) * normed).astype(BF16)
        ns[c, h] = normed
        rstds[c, h] = rstd
        yield

    def receive_grad(c, h):
        dout = og_buf[c, :, columns_of(h)].astype(F32)
        normed = ns[c, h]
        ngrad_ref[0, h : h + 1, :] += jnp.sum(dout * normed, axis=0, keepdims=True)
        dn = dout * gain_of(h)
        dz = rstds[c, h] * (dn - row_mean(dn) - normed * row_mean(dn * normed))
        dz2 = split(dz)
        put(dzs, c, h, dz2)
        yield
        back = product(stack(get(qes, c, h), get(ss, c, h), 1), dz2, TN)
        ls[c, h] = back[:width]
        v0s[c, h] = back[width:]
        yield

    def gradients(c, h):
        cols = columns_of(h)
        g2 = get(gs, c, h)
        kr2, w2, r2, dz2 = get(krs, c, h), get(ws, c, h), get(rs, c, h), get(dzs, c, h)
        v = v0s[c, h] + product(kr2, g2, NN)
        yield
        du = -product(get(ts, c, h), split(v), TN)
        yield
        both = stack(dz2, split(du), 0)
        inner = product(both, r2, NT)
        yield
        d2 = stack(split(-masks[0] * inner[:size]), split(-masks[1] * inner[size:]), 0)
        dqk = product(both, w2, NT) + product(d2, kr2, NN)
        yield
        dkr = product(d2, stack(get(qs, c, h), get(ks, c, h), 0), TN) - product(r2, g2, NT)
        yield
        sig, inv, k, base = sigs[c, h], invs[c, h], kf[c, h], base_of(h)
        rate_factor = sig * scale
        dk = dqk[size:] + (base * rate_factor) * dkr + du
        draw = inv * (dk - k * row_mean(dk * k))
        drate = jnp.sum(dkr * k, axis=-1, keepdims=True) * rate_factor
        rgrad_ref[:, h : h + 1] += jnp.sum(drate, axis=0, keepdims=True)
        dlogit = drate * base * (1.0 - sig)
        x = x_buf[c, :, cols]
        ggrad_ref[0, h : h + 1, :] += jnp.sum(dlogit * x.astype(F32), axis=0, keepdims=True)
        packed = split(cat([dqk[:size], draw, -du], 1))
        yield
        vgrad_ref[0, h] += dot(cat([x, x], 0), cat(packed, 0), TN)
        views = view_buf[h]
        dx = dot(packed[0], views, NT) + dot(packed[1], views, NT)
        dx = dx + og_buf[c, :, cols].astype(F32) + dlogit * gate_of(h)
        dx_buf[c, :, cols] = dx.astype(BF16)

    for ref in (vgrad_ref, ggrad_ref, rgrad_ref, ngrad_ref, igrad_ref):
        ref[...] = jnp.zeros_like(ref)

    all_heads = range(heads)

    pairing = 2 if count % 4 == 0 else 1
    by = range(pairing)

    def prepare_step(step, carry):
        chunks = [turn(step * pairing + i) for i in by]
        for c in chunks:
            arrived(x_buf, x_recv, c)
        together(prepare(c, h) for c in chunks for h in all_heads)
        return carry

    rounds = count // pairing
    half = rounds // 2
    lax.fori_loop(0, half, prepare_step, 0)
    for step in range(1, count):
        spread(og_ref, og_buf, og_send, og_recv, step).start()
    lax.fori_loop(half, rounds, prepare_step, 0)

    def advance(c, carry):
        for h in all_heads:
            w = init_buf[h]
            w2 = split(w)
            put(ws, c, h, w2)
            init_buf[h] = w - product(get(fs, c, h), w2, NN) + os_[c, h]
        return carry

    lax.fori_loop(0, count, advance, 0)

    def emit_step(step, carry):
        chunks = [turn(count - 1 - (step * pairing + i)) for i in by]
        together(emit(c, h) for c in chunks for h in all_heads)
        for c in chunks:
            collect(out_buf, next_ref, out_send, out_recv, c, after).start()
        return carry

    lax.fori_loop(0, rounds, emit_step, 0)

    def receive_step(step, carry):
        chunks = [turn(step * pairing + i) for i in by]
        for c in chunks:
            arrived(og_buf, og_recv, c)
        together(receive_grad(c, h) for c in chunks for h in all_heads)
        return carry

    lax.fori_loop(0, rounds, receive_step, 0)

    def retreat(step, carry):
        c = count - 1 - step
        for h in all_heads:
            g = igrad_ref[0, h]
            g2 = split(g)
            put(gs, c, h, g2)
            igrad_ref[0, h] = g - product(get(fs, c, h), g2, TN) + ls[c, h]
        return carry

    lax.fori_loop(0, count, retreat, 0)

    def gradient_step(step, carry):
        chunks = [turn(count - 1 - (step * pairing + i)) for i in by]
        together(gradients(c, h) for c in chunks for h in all_heads)
        for c in chunks:
            collect(dx_buf, prev_ref, dx_send, dx_recv, c, before_me).start()
        return carry

    lax.fori_loop(0, rounds, gradient_step, 0)

    for step in range(1, count):
        spread(x_ref, x_buf, x_send, x_recv, step).wait_send()
        spread(og_ref, og_buf, og_send, og_recv, step).wait_send()
    for c in range(count):
        collect(out_buf, next_ref, out_send, out_recv, c, after).wait_send()
        collect(dx_buf, prev_ref, dx_send, dx_recv, c, before_me).wait_send()
        collected(next_ref, out_recv, c)
        collected(prev_ref, dx_recv, c)


def hand_over(*refs):
    number = (len(refs) - 1) // 2
    copies = [pltpu.make_async_copy(refs[i], refs[number + i], refs[-1].at[i]) for i in range(number)]
    for copy in copies:
        copy.start()
    for copy in copies:
        copy.wait()


def per_device(segment_input, views, gate_vec, base_rate, norm_gain, init_weight, out_grad):
    count = lax.axis_size("ctx")
    size, features = segment_input.shape[1:]
    total, width = gate_vec.shape[1:]
    heads = total // count
    local = heads * width

    def shaped(shape, kind):
        return jax.ShapeDtypeStruct(shape, kind)

    vmem = pl.BlockSpec(memory_space=pltpu.VMEM)
    hbm = pl.BlockSpec(memory_space=pl.ANY)

    chunks = pltpu.VMEM((count, size, local), BF16)

    def pairs(rows, columns):
        return pltpu.VMEM((count, heads, 2, rows, columns), BF16)

    def floats(rows, columns):
        return pltpu.VMEM((count, heads, rows, columns), F32)

    results = pl.pallas_call(
        functools.partial(kernel, count, lax.axis_size("segment"), heads, size, width),
        out_shape=(
            shaped((1, size, features), BF16),
            shaped((1, heads, width, 3 * width), F32),
            shaped((1, heads, width), F32),
            shaped((1, heads), F32),
            shaped((1, heads, width), F32),
            shaped((1, heads, width, width), F32),
            shaped((1, size, features), BF16),
        ),
        in_specs=[hbm, hbm, hbm, vmem, vmem, vmem, hbm],
        out_specs=(hbm,) + (vmem,) * 5 + (hbm,),
        scratch_shapes=[
            pltpu.VMEM((heads, width, 3 * width), BF16),
            pltpu.VMEM((heads, width, width), F32),
            chunks, chunks, chunks, chunks,
            pltpu.VMEM((3 + levels_of(size), size, size), F32),
            pairs(size, width), pairs(size, width), pairs(size, width), pairs(size, width), pairs(size, width),
            pairs(size, size), pairs(size, size), pairs(width, width),
            pairs(size, width), pairs(size, width), pairs(width, width), pairs(width, width),
            floats(size, width), floats(size, width), floats(size, width), floats(width, width),
            floats(size, width), floats(width, width), floats(size, width),
            floats(size, 1), floats(size, 1), floats(size, 1),
            pltpu.SemaphoreType.DMA((2,)),
            *[pltpu.SemaphoreType.DMA((count,))] * 8,
        ],
        compiler_params=pltpu.CompilerParams(
            vmem_limit_bytes=56 * 1024 * 1024, collective_id=0, has_side_effects=True
        ),
    )(
        segment_input, out_grad, views, gate_vec, base_rate, norm_gain, init_weight
    )
    return pl.pallas_call(
        hand_over,
        out_shape=tuple(shaped(value.shape, value.dtype) for value in results),
        in_specs=[hbm] * len(results),
        out_specs=(vmem,) * len(results),
        scratch_shapes=[pltpu.SemaphoreType.DMA((len(results),))],
    )(*results)


def solution(mesh):
    return jax.shard_map(
        per_device,
        mesh=mesh,
        in_specs=(
            P("segment", "ctx", None),
            P("segment", None, None, None),
            P("segment", None, None),
            P("segment", None),
            P("segment", None, None),
            P("segment", None, None, None),
            P("segment", "ctx", None),
        ),
        out_specs=(
            P("segment", "ctx", None),
            P("segment", "ctx", None, None),
            P("segment", "ctx", None),
            P("segment", "ctx"),
            P("segment", "ctx", None),
            P("segment", "ctx", None, None),
            P("segment", "ctx", None),
        ),
        check_vma=False,
    )
```
